32 devices in a mesh: sx: 4 (over y, core), sy: 8 (over z, x).
Axes of the slice: x: 2, y: 2, z: 4, core: 2. Of those that a mesh axis runs over, the one named last changes fastest.
Arguments:
- basis: bfloat16 [4, 8, 8192, 512], P('sx', 'sy'), may hold values from -0.06629126 to 0.06629126
- diag_weight: float32 [4, 8, 8192], P('sx', 'sy'), may hold values from 0.5 to 4
- correlation_weight: float32 [4, 8, 2, 2048], P('sx', 'sy'), may hold values from 0.05 to 0.4
- tile_ids: int32 [4, 8, 4, 16], P('sx', 'sy'), may hold values from 0 to 63
- pair_live: int32 [4, 8, 2], replicated, may hold values 0 or 1
- loads: float32 [4, 8, 512, 256], P('sx', 'sy'), may hold values from -6 to 6
- load_count: int32 [4, 8], P('sx', 'sy'), may hold values from 1 to 256
Outputs:
- coeffs: float32 [4, 8, 512, 256], P('sx', 'sy')
The draws below stay inside these ranges and needn't reach their ends.
Inputs may be any that keep to these rules, and one draw needn't show every extreme that they name: Entries of pair_live for pairs beyond the grid's last column (index 0) or last row (index 1) are read by no step.
All inputs are finite; a program needn't handle non-finite values.
Results may differ from the reference program's by a relative error of at most 0.0015.
Values may be sent and summed in bfloat16 or wider, within the bound.
A program may use at most 128 MiB of HBM per device.

```python
import math
import jax
import jax.numpy as jnp
from jax import lax

K = 512
L = 256
TILE = 128
RT = 64
NT = 16
ITERS = 3
R = 8192
OV = 2048
N_SX = 4
N_SY = 8


def draw_basis(key, part):
    spread_scale = R ** (-0.5)
    odd_columns = jnp.arange(K, dtype=jnp.int32) % 2 == 1

    def one_block(block_index):
        block_key = jax.random.fold_in(jax.random.fold_in(key, 7031), block_index)
        fresh_key, extra_key, chosen_key = jax.random.split(block_key, 3)
        fresh_part = jax.random.normal(fresh_key, (R, K), jnp.float32)
        extra_part = jax.random.normal(extra_key, (R, K), jnp.float32)
        chosen = jnp.logical_and(jax.random.randint(chosen_key, (K,), 0, 8) == 0, odd_columns)
        copied = (jnp.roll(fresh_part, 1, axis=1) + 0.5 * extra_part) / 1.118034
        mixed_block = jnp.where(chosen[None, :], copied, fresh_part)
        return (jnp.clip(mixed_block, -6.0, 6.0) * spread_scale).astype(jnp.bfloat16)
    blocks = lax.map(one_block, jnp.arange(N_SX * N_SY, dtype=jnp.int32))
    return blocks.reshape(N_SX, N_SY, R, K)


def draw_correlation_weight(key, part):
    full_shape = (N_SX, N_SY, 2, OV)
    base_key = jax.random.fold_in(key, 9127)
    uniform_part = jax.random.uniform(base_key, full_shape, jnp.float32, 0.0, 1.0)
    return jnp.clip(0.05 * jnp.exp(uniform_part * jnp.log(8.0)), 0.05, 0.4)


def touch_ends(array, key, smallest, high):
    dims = array.shape
    place = [jax.random.randint(jax.random.fold_in(key, axis), (), 0, dims[axis]) for axis in range(len(dims))]
    array = array.at[tuple(place)].set(smallest)
    longest = dims.index(max(dims))
    place[longest] = (place[longest] + 1) % dims[longest]
    return array.at[tuple(place)].set(high)


def level_of(rng, shape, cuts, least, top_value):
    gain, own = 1.0, jax.random.fold_in(rng, 6)
    for axis_at, shards_of in cuts:
        heights = jnp.exp(jax.random.uniform(jax.random.fold_in(own, axis_at), (shards_of,), jnp.float32, least / len(cuts), top_value / len(cuts)))
        gain = gain * jnp.repeat(heights, shape[axis_at] // shards_of).reshape([-1 if axis == axis_at else 1 for axis in range(len(shape))])
    return gain


def bell_draw(rng, dims, deviation, limit, cuts=(), held_as=jnp.bfloat16):
    drawn = deviation * jax.random.normal(rng, dims, jnp.float32)
    if cuts:
        drawn = drawn * level_of(rng, dims, cuts, -0.22, 0.18)
    return jnp.clip(drawn, -limit, limit).astype(held_as)


def setup_inputs(seed: int = 0) -> dict:
    key_of = jax.random.split(jax.random.key(seed), 8)
    basis = draw_basis(jax.random.fold_in(key_of[7], 71), 0)
    diag_weight = jnp.clip(jnp.exp(math.log(4.0) - 2.0794415 * jax.random.uniform(key_of[1], (N_SX, N_SY, R), jnp.float32) ** level_of(key_of[1], (N_SX, N_SY, R), ((0, 4), (1, 8)), -0.2, 0.2)), 0.5, 4.0)
    correlation_weight = draw_correlation_weight(jax.random.fold_in(key_of[7], 71), 0)
    tile_ids = touch_ends(jax.random.randint(key_of[3], (N_SX, N_SY, 4, NT), 0, RT), jax.random.fold_in(key_of[3], 1), 0, RT - 1).astype(jnp.int32)
    pair_live = touch_ends((jax.random.randint(key_of[4], (N_SX, N_SY, 2), 0, 4) < 3).astype(jnp.int32), jax.random.fold_in(key_of[4], 1), 0, 1)
    loads = bell_draw(key_of[5], (N_SX, N_SY, K, L), 1.0, 6.0, ((0, 4), (1, 8)), jnp.float32)
    load_count = touch_ends(jax.random.randint(key_of[6], (N_SX, N_SY), 1, L + 1), jax.random.fold_in(key_of[6], 1), 1, L).astype(jnp.int32)
    return {"basis": basis, "diag_weight": diag_weight, "correlation_weight": correlation_weight, "tile_ids": tile_ids, "pair_live": pair_live, "loads": loads, "load_count": load_count}


damping = 0.8

def stencil(rows_in, weight):
    values = rows_in.astype(jnp.float32)
    zero_row = jnp.zeros_like(values[:1])
    before = jnp.concatenate([zero_row, values[:-1]], axis=0)
    after = jnp.concatenate([values[1:], zero_row], axis=0)
    return weight[:, None] * (2.5 * values - before - after)

def interface(local_basis, tile_list):
    tiled = local_basis.reshape(-1, TILE, local_basis.shape[1])
    return jnp.take(tiled, tile_list.astype(jnp.int32), axis=0).reshape(-1, local_basis.shape[1])

def contract(left_rows, right_rows):
    return lax.dot_general(left_rows.astype(jnp.float32), right_rows.astype(jnp.float32), (((0,), (0,)), ((), ())), preferred_element_type=jnp.float32)

def apply_blocks(blocks, vectors):
    return jnp.einsum('abkm,abml->abkl', blocks, vectors, precision=lax.Precision.HIGHEST)

def mirror_blocks(blocks, vectors):
    return jnp.einsum('abmk,abml->abkl', blocks, vectors, precision=lax.Precision.HIGHEST)

def reference(basis, diag_weight, correlation_weight, tile_ids, pair_live, loads, load_count):

    def per_device(device):
        row_at = device // N_SY
        col_at = device % N_SY
        col_next = jnp.minimum(col_at + 1, N_SY - 1)
        row_next = jnp.minimum(row_at + 1, N_SX - 1)
        local_basis = basis[row_at, col_at]
        weighted = (diag_weight[row_at, col_at][:, None] * local_basis.astype(jnp.float32)).astype(jnp.bfloat16)
        diagonal_block = contract(local_basis, weighted)
        image_east = stencil(interface(basis[row_at, col_next], tile_ids[row_at, col_next, 0]), correlation_weight[row_at, col_next, 0]).astype(jnp.bfloat16)
        live_east = (pair_live[row_at, col_at, 0] * (col_at < N_SY - 1)).astype(jnp.float32)
        block_east = contract(interface(local_basis, tile_ids[row_at, col_at, 1]), image_east) * live_east
        image_south = stencil(interface(basis[row_next, col_at], tile_ids[row_next, col_at, 2]), correlation_weight[row_next, col_at, 1]).astype(jnp.bfloat16)
        live_south = (pair_live[row_at, col_at, 1] * (row_at < N_SX - 1)).astype(jnp.float32)
        block_south = contract(interface(local_basis, tile_ids[row_at, col_at, 3]), image_south) * live_south
        return (diagonal_block, block_east, block_south)
    diagonal, east, south = lax.map(per_device, jnp.arange(N_SX * N_SY, dtype=jnp.int32))
    diagonal = diagonal.reshape(N_SX, N_SY, K, K)
    east = east.reshape(N_SX, N_SY, K, K)
    south = south.reshape(N_SX, N_SY, K, K)
    factor = jnp.linalg.cholesky(diagonal)
    live_cols = (jnp.arange(L, dtype=jnp.int32)[None, None, :] < load_count[:, :, None]).astype(jnp.float32)
    rhs = loads * live_cols[:, :, None, :]
    coeffs = damping * jax.scipy.linalg.cho_solve((factor, True), rhs)
    block_west = jnp.concatenate([jnp.zeros_like(east[:, :1]), east[:, :-1]], axis=1)
    block_north = jnp.concatenate([jnp.zeros_like(south[:1]), south[:-1]], axis=0)
    for sweep in range(1, ITERS):
        from_east = jnp.concatenate([coeffs[:, 1:], jnp.zeros_like(coeffs[:, :1])], axis=1)
        from_west = jnp.concatenate([jnp.zeros_like(coeffs[:, :1]), coeffs[:, :-1]], axis=1)
        from_south = jnp.concatenate([coeffs[1:], jnp.zeros_like(coeffs[:1])], axis=0)
        from_north = jnp.concatenate([jnp.zeros_like(coeffs[:1]), coeffs[:-1]], axis=0)
        residual = rhs - apply_blocks(diagonal, coeffs) - apply_blocks(east, from_east) - apply_blocks(south, from_south)
        residual = residual - mirror_blocks(block_west, from_west) - mirror_blocks(block_north, from_north)
        coeffs = coeffs + damping * jax.scipy.linalg.cho_solve((factor, True), residual)
    return coeffs
```

```python
import functools

import jax
import jax.numpy as jnp
from jax import lax
from jax.experimental import pallas as pl
from jax.experimental.pallas import tpu as pltpu
from jax.sharding import PartitionSpec as P

TILE = 128
ITERS = 3
HALO = 16
damping = 0.8
MESH = pl.DeviceIdType.MESH
F32 = jnp.float32
BF16 = jnp.bfloat16
VMEM = pl.BlockSpec(memory_space=pltpu.VMEM)
SMEM = pl.BlockSpec(memory_space=pltpu.SMEM)
ANY = pl.BlockSpec(memory_space=pl.ANY)


def dot(a, b):
    return jnp.dot(a, b, preferred_element_type=F32)


def dot_t(a, b):
    return lax.dot_general(a, b, (((0,), (0,)), ((), ())), preferred_element_type=F32)


def split(a):
    high = a.astype(BF16)
    return high, (a - high.astype(F32)).astype(BF16)


def dot3(a, b):
    return dot(a[0], b[0]) + (dot(a[0], b[1]) + dot(a[1], b[0]))


def tile_copy(ids_ref, side, basis_ref, rows_ref, offset, sems, t):
    return pltpu.make_async_copy(
        basis_ref.at[pl.ds(pl.multiple_of(ids_ref[side, t] * TILE, TILE), TILE), :],
        rows_ref.at[pl.ds(offset + t * TILE, TILE), :],
        sems.at[t],
    )


def image_kernel(side, ids_ref, basis_ref, weight_ref, out_ref, rows_ref, sems):
    tiles = out_ref.shape[0] // TILE
    width = out_ref.shape[1]
    for t in range(tiles):
        tile_copy(ids_ref, side, basis_ref, rows_ref, HALO, sems, t).start()
    zero = jnp.zeros((HALO, width), BF16)
    rows_ref[pl.ds(0, HALO), :] = zero
    rows_ref[pl.ds(HALO + tiles * TILE, HALO), :] = zero
    for t in range(tiles):
        tile_copy(ids_ref, side, basis_ref, rows_ref, HALO, sems, t).wait()

    @pl.loop(0, tiles)
    def _(t):
        start = pl.multiple_of(t * TILE, TILE)
        values = rows_ref[pl.ds(start, TILE + 2 * HALO), :].astype(F32)
        scale = jnp.broadcast_to(weight_ref[pl.ds(t, 1), :], (TILE, TILE)).T
        scale = jnp.concatenate([scale] * (width // TILE), axis=1)
        here = values[HALO : HALO + TILE]
        before = values[HALO - 1 : HALO - 1 + TILE]
        after = values[HALO + 1 : HALO + 1 + TILE]
        out_ref[pl.ds(start, TILE), :] = (scale * (2.5 * here - before - after)).astype(BF16)


def image_of(side, tile_ids, basis, weight):
    rows, width = weight.shape[0], basis.shape[1]
    tiles = rows // TILE
    return pl.pallas_call(
        functools.partial(image_kernel, side),
        out_shape=jax.ShapeDtypeStruct((rows, width), BF16),
        in_specs=[SMEM, ANY, VMEM],
        out_specs=VMEM,
        scratch_shapes=[
            pltpu.VMEM((rows + 2 * HALO, width), BF16),
            pltpu.SemaphoreType.DMA((tiles,)),
        ],
        cost_estimate=pl.CostEstimate(
            flops=8 * rows * width, bytes_accessed=4 * rows * width, transcendentals=0
        ),
        name="image",
    )(tile_ids, basis, weight.reshape(tiles, TILE))


def block_kernel(side, ids_ref, live_ref, basis_ref, image_ref, out_ref, rows_ref, sems):
    tiles = rows_ref.shape[0] // TILE
    for t in range(tiles):
        tile_copy(ids_ref, side, basis_ref, rows_ref, 0, sems, t).start()
    for t in range(tiles):
        tile_copy(ids_ref, side, basis_ref, rows_ref, 0, sems, t).wait()
    block = dot_t(rows_ref[...], image_ref[...])
    live = jnp.full(block.shape, live_ref[0], jnp.int32) > 0
    out_ref[...] = jnp.where(live, block, 0.0).astype(BF16)


def block_of(side, tile_ids, live, basis, image):
    rows, width = image.shape
    tiles = rows // TILE
    return pl.pallas_call(
        functools.partial(block_kernel, side),
        out_shape=jax.ShapeDtypeStruct((width, width), BF16),
        in_specs=[SMEM, SMEM, ANY, VMEM],
        out_specs=VMEM,
        scratch_shapes=[
            pltpu.VMEM((rows, width), BF16),
            pltpu.SemaphoreType.DMA((tiles,)),
        ],
        cost_estimate=pl.CostEstimate(
            flops=2 * rows * width * width, bytes_accessed=4 * rows * width, transcendentals=0
        ),
        name="block",
    )(tile_ids, live.astype(jnp.int32).reshape(1), basis, image)


def diagonal_kernel(count_ref, basis_ref, weight_ref, loads_ref, inv_ref, first_ref, a_ref, x_ref):
    step = pl.program_id(0)
    width = a_ref.shape[0]
    half = width // 2

    @pl.when(step == 0)
    def _():
        a_ref[...] = jnp.zeros_like(a_ref)

    rows = basis_ref[...]
    turned = rows.T
    pieces = []
    for t in range(weight_ref.shape[0]):
        piece = turned[:, t * TILE : (t + 1) * TILE].astype(F32)
        pieces.append((piece * weight_ref[pl.ds(t, 1), :]).astype(BF16))
    weighted = jnp.concatenate(pieces, axis=1)
    a_ref[:half, :] += dot(weighted[:half], rows)
    a_ref[half:, half:] += dot(weighted[half:], rows[:, half:])

    @pl.when(step == pl.num_programs(0) - 1)
    def _():
        a_ref[half:, :half] = a_ref[:half, half:].T
        a = a_ref[...]
        row_at = lax.broadcasted_iota(jnp.int32, a.shape, 0)
        col_at = lax.broadcasted_iota(jnp.int32, a.shape, 1)
        eye = jnp.where(row_at == col_at, 1.0, 0.0).astype(F32)
        bound = jnp.max(jnp.sum(jnp.abs(a), axis=0, keepdims=True))
        split_a = split(a)
        low = 0.004
        scale = 2.0 / (1.0 + low)
        alpha = scale / bound
        low = scale * low
        low = 1.0 - (1.0 - low) ** 2
        scale = 2.0 / (1.0 + low)
        low = scale * low
        x_ref[...] = scale * alpha * (2.0 * eye - alpha * a)

        def coarse(i, low):
            low = low * (2.0 - low)
            scale = 2.0 / (1.0 + low)
            x = x_ref[...]
            xb = x.astype(BF16)
            t = dot(split_a[0], xb)
            x_ref[...] = scale * (2.0 * x - dot(xb, t.astype(BF16)))
            return low * scale

        lax.fori_loop(0, 5, coarse, jnp.float32(low))

        def fine(state):
            i, _ = state
            x = x_ref[...]
            split_x = split(x)
            r = eye - dot3(split_a, split_x)
            size = jnp.sum(r * r)
            moved = x + dot3(split_x, split(r))
            restart = jnp.logical_and(i == 0, jnp.logical_not(size < 1.0))
            take = jnp.full(x.shape, restart.astype(jnp.int32), jnp.int32) > 0
            x_ref[...] = jnp.where(take, eye / bound, moved)
            return i + 1, size

        lax.while_loop(
            lambda s: jnp.logical_and(
                s[0] < 48, jnp.logical_or(s[0] < 2 - (s[1] < 1.0).astype(jnp.int32), s[1] >= 0.01)
            ),
            fine,
            (jnp.int32(0), jnp.float32(1.0)),
        )
        inverse = x_ref[...].astype(BF16)
        inv_ref[...] = inverse
        loads = loads_ref[...]
        column = lax.broadcasted_iota(jnp.int32, loads.shape, 1)
        rhs = jnp.where(column < count_ref[0], loads, 0.0)
        y = dot(inverse, rhs.astype(BF16))
        y = y + dot(inverse, (rhs - dot3(split_a, split(y))).astype(BF16))
        first_ref[...] = damping * y


def diagonal_of(count, basis, weight, loads):
    rows, width = basis.shape
    columns = loads.shape[1]
    chunk = 1024
    return pl.pallas_call(
        diagonal_kernel,
        grid=(rows // chunk,),
        out_shape=(
            jax.ShapeDtypeStruct((width, width), BF16),
            jax.ShapeDtypeStruct((width, columns), F32),
        ),
        in_specs=[
            SMEM,
            pl.BlockSpec((chunk, width), lambda i: (i, 0)),
            pl.BlockSpec((chunk // TILE, TILE), lambda i: (i, 0)),
            pl.BlockSpec((width, columns), lambda i: (0, 0)),
        ],
        out_specs=(
            pl.BlockSpec((width, width), lambda i: (0, 0)),
            pl.BlockSpec((width, columns), lambda i: (0, 0)),
        ),
        scratch_shapes=[pltpu.VMEM((width, width), F32), pltpu.VMEM((width, width), F32)],
        compiler_params=pltpu.CompilerParams(dimension_semantics=("arbitrary",)),
        cost_estimate=pl.CostEstimate(
            flops=2 * rows * width * width + 40 * width**3,
            bytes_accessed=2 * rows * width,
            transcendentals=0,
        ),
        name="diagonal",
    )(count, basis, weight.reshape(rows // TILE, TILE), loads)


def sweep_kernel(
    n_sx, n_sy, inv_ref, first_ref, east_ref, south_ref, out_ref, own, for_east, for_south,
    got, total, send_sem, recv_sem,
):
    row, col = lax.axis_index("sx"), lax.axis_index("sy")
    west = (col > 0, (row, col - 1))
    north = (row > 0, (row - 1, col))
    east = (col < n_sy - 1, (row, col + 1))
    south = (row < n_sx - 1, (row + 1, col))
    sides = (west, north, east, south)
    barrier = pltpu.get_barrier_semaphore()
    present = jnp.int32(0)
    for there, place in sides:
        present = present + there.astype(jnp.int32)

        @pl.when(there)
        def _():
            pl.semaphore_signal(barrier, inc=1, device_id=place, device_id_type=MESH)

    pl.semaphore_wait(barrier, present)

    def copy_to(sweep, side):
        source = (own, own, for_east, for_south)[side]
        return pltpu.make_async_remote_copy(
            src_ref=source.at[sweep],
            dst_ref=got.at[sweep, (side + 2) % 4],
            send_sem=send_sem.at[sweep, side],
            recv_sem=recv_sem.at[sweep, (side + 2) % 4],
            device_id=sides[side][1],
            device_id_type=MESH,
        )

    def arrival(sweep, side):
        return pltpu.make_async_remote_copy(
            src_ref=got.at[sweep, side],
            dst_ref=got.at[sweep, side],
            send_sem=send_sem.at[sweep, side],
            recv_sem=recv_sem.at[sweep, side],
            device_id=sides[side][1],
            device_id_type=MESH,
        )

    def send(sweep, side):
        @pl.when(sides[side][0])
        def _():
            copy_to(sweep, side).start()

    out_ref[...] = first_ref[...]
    for sweep in range(ITERS - 1):
        coeffs = out_ref[...].astype(BF16)
        own[sweep] = coeffs
        for_east[sweep] = dot_t(east_ref[...], coeffs).astype(BF16)
        send(sweep, 0)
        send(sweep, 1)
        for_south[sweep] = dot_t(south_ref[...], coeffs).astype(BF16)
        send(sweep, 2)
        send(sweep, 3)
        total[...] = jnp.zeros_like(total)
        for side in (1, 3, 0, 2):
            @pl.when(sides[side][0])
            def _():
                arrival(sweep, side).wait_recv()
                value = got[sweep, side]
                if side == 2:
                    total[...] += dot(east_ref[...], value)
                elif side == 3:
                    total[...] += dot(south_ref[...], value)
                else:
                    total[...] += value.astype(F32)

        out_ref[...] = (
            (1.0 - damping) * out_ref[...]
            + first_ref[...]
            - damping * dot(inv_ref[...], total[...].astype(BF16))
        )
    for sweep in range(ITERS - 1):
        for side in range(4):
            @pl.when(sides[side][0])
            def _():
                copy_to(sweep, side).wait_send()


def sweeps_of(n_sx, n_sy, inverse, first, east, south):
    shape = first.shape
    further = ITERS - 1
    return pl.pallas_call(
        functools.partial(sweep_kernel, n_sx, n_sy),
        out_shape=jax.ShapeDtypeStruct(shape, F32),
        in_specs=[VMEM] * 4,
        out_specs=VMEM,
        scratch_shapes=[
            pltpu.VMEM((further,) + shape, BF16),
            pltpu.VMEM((further,) + shape, BF16),
            pltpu.VMEM((further,) + shape, BF16),
            pltpu.VMEM((further, 4) + shape, BF16),
            pltpu.VMEM(shape, F32),
            pltpu.SemaphoreType.DMA((further, 4)),
            pltpu.SemaphoreType.DMA((further, 4)),
        ],
        compiler_params=pltpu.CompilerParams(collective_id=0, has_side_effects=True),
        name="sweeps",
    )(inverse, first, east, south)


def moved_back(block, axis, peers):
    return lax.ppermute(block, axis, [(i + 1, i) for i in range(peers - 1)])


def solution(mesh):
    n_sx, n_sy = mesh.shape["sx"], mesh.shape["sy"]

    def on_device(basis, diag_weight, correlation_weight, tile_ids, pair_live, loads, load_count):
        basis = basis[0, 0]
        ids = tile_ids[0, 0]
        row_at, col_at = lax.axis_index("sx"), lax.axis_index("sy")
        live = pair_live[row_at, col_at]
        live_east = jnp.logical_and(live[0] > 0, col_at < n_sy - 1)
        live_south = jnp.logical_and(live[1] > 0, row_at < n_sx - 1)
        image_west = image_of(0, ids, basis, correlation_weight[0, 0, 0])
        from_east = moved_back(image_west, "sy", n_sy)
        image_north = image_of(2, ids, basis, correlation_weight[0, 0, 1])
        from_south = moved_back(image_north, "sx", n_sx)
        inverse, first = diagonal_of(load_count[0], basis, diag_weight[0, 0], loads[0, 0])
        block_south = block_of(3, ids, live_south, basis, from_south)
        block_east = block_of(1, ids, live_east, basis, from_east)
        coeffs = sweeps_of(n_sx, n_sy, inverse, first, block_east, block_south)
        return coeffs[None, None]

    return jax.shard_map(
        on_device,
        mesh=mesh,
        in_specs=(
            P("sx", "sy", None, None),
            P("sx", "sy", None),
            P("sx", "sy", None, None),
            P("sx", "sy", None, None),
            P(),
            P("sx", "sy", None, None),
            P("sx", "sy"),
        ),
        out_specs=P("sx", "sy", None, None),
        check_vma=False,
    )
```

```python
import functools

import jax
import jax.numpy as jnp
from jax import lax
from jax.experimental import pallas as pl
from jax.experimental.pallas import tpu as pltpu
from jax.sharding import PartitionSpec as P

TILE = 128
ITERS = 3
HALO = 16
damping = 0.8
MESH = pl.DeviceIdType.MESH
F32 = jnp.float32
BF16 = jnp.bfloat16
VMEM = pl.BlockSpec(memory_space=pltpu.VMEM)
SMEM = pl.BlockSpec(memory_space=pltpu.SMEM)
ANY = pl.BlockSpec(memory_space=pl.ANY)


def dot(a, b):
    return jnp.dot(a, b, preferred_element_type=F32)


def dot_t(a, b):
    return lax.dot_general(a, b, (((0,), (0,)), ((), ())), preferred_element_type=F32)


def split(a):
    high = a.astype(BF16)
    return high, (a - high.astype(F32)).astype(BF16)


def dot3(a, b):
    return dot(a[0], b[0]) + (dot(a[0], b[1]) + dot(a[1], b[0]))


def tile_of(basis_ref, ids_ref, side, t):
    return basis_ref[ids_ref[side, t]]


def image_tile(basis_ref, ids_ref, side, t, tiles, scale):
    width = basis_ref.shape[2]
    scale = jnp.broadcast_to(scale, (TILE, TILE)).T
    scale = jnp.concatenate([scale] * (width // TILE), axis=1)
    before = ids_ref[side, lax.rem(t + tiles - 1, tiles)]
    after = ids_ref[side, lax.rem(t + 1, tiles)]
    first = basis_ref[before, TILE - HALO :, :].astype(F32)
    last = basis_ref[after, :HALO, :].astype(F32)
    first = first * (t > 0).astype(F32)
    last = last * (t < tiles - 1).astype(F32)
    here = tile_of(basis_ref, ids_ref, side, t).astype(F32)
    values = jnp.concatenate([first, here, last], axis=0)
    before = values[HALO - 1 : HALO - 1 + TILE]
    after = values[HALO + 1 : HALO + 1 + TILE]
    return (scale * (2.5 * here - before - after)).astype(BF16)


def eye_like(a):
    row_at = lax.broadcasted_iota(jnp.int32, a.shape, 0)
    col_at = lax.broadcasted_iota(jnp.int32, a.shape, 1)
    return jnp.where(row_at == col_at, 1.0, 0.0).astype(F32)


def norm_bound(a):
    return jnp.max(jnp.sum(jnp.abs(a), axis=0, keepdims=True), axis=1, keepdims=True)


def fine_step(split_a, x):
    split_x = split(x)
    r = eye_like(x) - dot3(split_a, split_x)
    return x + dot3(split_x, split(r)), jnp.sum(r * r, axis=0, keepdims=True)


def first_coeffs(split_a, inverse, loads, carried):
    rhs = loads * carried
    y = dot(inverse, rhs.astype(BF16))
    y = y + dot(inverse, (rhs - dot3(split_a, split(y))).astype(BF16))
    return damping * y


def neighbours(n_sx, n_sy):
    row, col = lax.axis_index("sx"), lax.axis_index("sy")
    west = (col > 0, (row, col - 1))
    north = (row > 0, (row - 1, col))
    east = (col < n_sy - 1, (row, col + 1))
    south = (row < n_sx - 1, (row + 1, col))
    return west, north, east, south


def meet(sides):
    barrier = pltpu.get_barrier_semaphore()
    present = jnp.int32(0)
    for there, place in sides:
        present = present + there.astype(jnp.int32)

        @pl.when(there)
        def _():
            pl.semaphore_signal(barrier, inc=1, device_id=place, device_id_type=MESH)

    pl.semaphore_wait(barrier, present)


def assemble_kernel(
    n_sx, n_sy, ids_ref, live_ref, count_ref, basis_ref, corr_ref, weight_ref, loads_ref,
    a_out, x_out, size_ref, inv_ref, first_ref, east_ref, south_ref,
    a_ref, x_ref, block_ref, sent, got, send_sem, recv_sem, local_sem,
):
    rows, width = basis_ref.shape[0] * TILE, basis_ref.shape[2]
    half = width // 2
    tiles = corr_ref.shape[1]
    per = 2 if tiles % 2 == 0 else 1
    chunk = per * TILE
    chunks = tiles // per
    sides = neighbours(n_sx, n_sy)
    meet(sides)

    def piece(which, q, peer):
        at = pl.ds(pl.multiple_of(q * chunk, chunk), chunk)
        return pltpu.make_async_remote_copy(
            src_ref=sent.at[which, at, :],
            dst_ref=got.at[which, at, :],
            send_sem=send_sem.at[which, q],
            recv_sem=recv_sem.at[which, q],
            device_id=sides[peer][1],
            device_id_type=MESH,
        )

    for which in range(2):

        @pl.when(sides[which][0])
        def _():
            @pl.loop(0, chunks)
            def _(q):
                for k in range(per):
                    t = q * per + k
                    at = pl.ds(pl.multiple_of(t * TILE, TILE), TILE)
                    sent[which, at, :] = image_tile(
                        basis_ref, ids_ref, 2 * which, t, tiles, corr_ref[which, pl.ds(t, 1), :]
                    )
                piece(which, q, which).start()

    a_ref[...] = jnp.zeros_like(a_ref)
    step_tiles = 8
    step_rows = step_tiles * TILE

    @pl.loop(0, rows // step_rows)
    def _(i):
        part = basis_ref[pl.ds(i * step_tiles, step_tiles)].reshape(step_rows, width)
        scale = weight_ref[pl.ds(pl.multiple_of(i * step_tiles, step_tiles), step_tiles), :]
        turned = part.T
        pieces = []
        for t in range(step_tiles):
            tile = turned[:, t * TILE : (t + 1) * TILE].astype(F32)
            pieces.append((tile * scale[t : t + 1, :]).astype(BF16))
        weighted = jnp.concatenate(pieces, axis=1)
        a_ref[:half, :] += dot(weighted[:half], part)
        a_ref[half:, half:] += dot(weighted[half:], part[:, half:])

    a_ref[half:, :half] = a_ref[:half, half:].T
    a_copy = pltpu.make_async_copy(a_ref, a_out, local_sem.at[0])
    a_copy.start()
    a = a_ref[...]
    bound = norm_bound(a)
    split_a = split(a)
    low = 0.004
    scale = 2.0 / (1.0 + low)
    alpha = scale / bound
    low = scale * low
    low = low * (2.0 - low)
    scale = 2.0 / (1.0 + low)
    low = scale * low
    x_ref[...] = (scale * alpha) * (2.0 * eye_like(a) - alpha * a)

    def coarse(i, low):
        low = low * (2.0 - low)
        scale = 2.0 / (1.0 + low)
        x = x_ref[...]
        xb = x.astype(BF16)
        t = dot(split_a[0], xb)
        x_ref[...] = scale * (2.0 * x - dot(xb, t.astype(BF16)))
        return low * scale

    lax.fori_loop(0, 5, coarse, jnp.float32(low))

    @pl.loop(0, 2)
    def _(i):
        x, size = fine_step(split_a, x_ref[...])
        x_ref[...] = x
        size_ref[...] = size

    x_copy = pltpu.make_async_copy(x_ref, x_out, local_sem.at[1])
    x_copy.start()
    inverse = x_ref[...].astype(BF16)
    inv_ref[...] = inverse
    first_ref[...] = first_coeffs(split_a, inverse, loads_ref[...], count_ref[...])

    for which, out_ref in ((1, south_ref), (0, east_ref)):
        block_ref[...] = jnp.zeros_like(block_ref)

        @pl.when(sides[which + 2][0])
        def _():
            @pl.loop(0, chunks)
            def _(q):
                piece(which, q, which + 2).wait_recv()
                at = pl.ds(pl.multiple_of(q * chunk, chunk), chunk)
                mine = jnp.concatenate(
                    [
                        tile_of(basis_ref, ids_ref, 2 * which + 1, q * per + k)
                        for k in range(per)
                    ],
                    axis=0,
                )
                block_ref[...] += dot_t(mine, got[which, at, :])

        out_ref[...] = (block_ref[...] * live_ref[which]).astype(BF16)

    for which in range(2):

        @pl.when(sides[which][0])
        def _():
            @pl.loop(0, chunks)
            def _(q):
                piece(which, q, which).wait_send()

    a_copy.wait()
    x_copy.wait()


def assemble(n_sx, n_sy, ids, live, count, basis, corr, weight, loads):
    rows, width = basis.shape
    overlap = corr.shape[1]
    tiles = overlap // TILE
    chunks = tiles // 2 if tiles % 2 == 0 else tiles
    square = jax.ShapeDtypeStruct((width, width), F32)
    short = jax.ShapeDtypeStruct((width, width), BF16)
    return pl.pallas_call(
        functools.partial(assemble_kernel, n_sx, n_sy),
        out_shape=(
            square, square, jax.ShapeDtypeStruct((1, width), F32), short,
            jax.ShapeDtypeStruct(loads.shape, F32), short, short,
        ),
        in_specs=[SMEM, SMEM, VMEM, VMEM, VMEM, VMEM, VMEM],
        out_specs=(ANY, ANY, VMEM, VMEM, VMEM, VMEM, VMEM),
        scratch_shapes=[
            pltpu.VMEM((width, width), F32),
            pltpu.VMEM((width, width), F32),
            pltpu.VMEM((width, width), F32),
            pltpu.VMEM((2, overlap, width), BF16),
            pltpu.VMEM((2, overlap, width), BF16),
            pltpu.SemaphoreType.DMA((2, chunks)),
            pltpu.SemaphoreType.DMA((2, chunks)),
            pltpu.SemaphoreType.DMA((2,)),
        ],
        compiler_params=pltpu.CompilerParams(collective_id=1, has_side_effects=True),
        name="assemble",
    )(
        ids, live, count, basis.reshape(rows // TILE, TILE, width), corr.reshape(2, tiles, TILE),
        weight.reshape(rows // TILE, TILE), loads,
    )


def finish_kernel(
    count_ref, size_ref, a_hbm, x_hbm, loads_hbm, inv_in, first_in, inv_out, first_out,
    a_ref, x_ref, loads_ref, inv_ref, first_ref, sems,
):
    size = jnp.sum(size_ref[...])

    @pl.when(jnp.logical_not(size < 0.01))
    def _():
        inputs = [
            pltpu.make_async_copy(source, target, sems.at[k])
            for k, (source, target) in enumerate(
                ((a_hbm, a_ref), (x_hbm, x_ref), (loads_hbm, loads_ref))
            )
        ]
        for copy in inputs:
            copy.start()
        for copy in inputs:
            copy.wait()
        a = a_ref[...]
        split_a = split(a)

        @pl.when(jnp.logical_not(size < 1.0))
        def _():
            x_ref[...] = eye_like(a) / norm_bound(a)

        def step(state):
            i, _ = state
            x, size = fine_step(split_a, x_ref[...])
            x_ref[...] = x
            return i + 1, jnp.sum(size)

        lax.while_loop(
            lambda s: jnp.logical_and(s[0] < 48, s[1] >= 0.0001),
            step,
            (jnp.int32(0), jnp.float32(1.0)),
        )
        inverse = x_ref[...].astype(BF16)
        inv_ref[...] = inverse
        first_ref[...] = first_coeffs(split_a, inverse, loads_ref[...], count_ref[...])
        outputs = [
            pltpu.make_async_copy(inv_ref, inv_out, sems.at[3]),
            pltpu.make_async_copy(first_ref, first_out, sems.at[4]),
        ]
        for copy in outputs:
            copy.start()
        for copy in outputs:
            copy.wait()


def finish(count, size, a, x, loads, inverse, first):
    square = pltpu.VMEM(a.shape, F32)
    return pl.pallas_call(
        finish_kernel,
        out_shape=(
            jax.ShapeDtypeStruct(inverse.shape, BF16), jax.ShapeDtypeStruct(first.shape, F32),
        ),
        in_specs=[VMEM, VMEM, ANY, ANY, ANY, ANY, ANY],
        out_specs=(ANY, ANY),
        scratch_shapes=[
            square, square, pltpu.VMEM(loads.shape, F32), pltpu.VMEM(inverse.shape, BF16),
            pltpu.VMEM(first.shape, F32), pltpu.SemaphoreType.DMA((5,)),
        ],
        input_output_aliases={5: 0, 6: 1},
        name="finish",
    )(count, size, a, x, loads, inverse, first)


def sweep_kernel(
    n_sx, n_sy, inv_ref, first_ref, east_ref, south_ref, out_ref, own, for_east, for_south,
    got, total, send_sem, recv_sem,
):
    sides = neighbours(n_sx, n_sy)
    meet(sides)

    def copy_to(sweep, side):
        source = (own, own, for_east, for_south)[side]
        return pltpu.make_async_remote_copy(
            src_ref=source.at[sweep],
            dst_ref=got.at[sweep, (side + 2) % 4],
            send_sem=send_sem.at[sweep, side],
            recv_sem=recv_sem.at[sweep, (side + 2) % 4],
            device_id=sides[side][1],
            device_id_type=MESH,
        )

    def arrival(sweep, side):
        return pltpu.make_async_remote_copy(
            src_ref=got.at[sweep, side],
            dst_ref=got.at[sweep, side],
            send_sem=send_sem.at[sweep, side],
            recv_sem=recv_sem.at[sweep, side],
            device_id=sides[side][1],
            device_id_type=MESH,
        )

    def send(sweep, side):
        @pl.when(sides[side][0])
        def _():
            copy_to(sweep, side).start()

    out_ref[...] = first_ref[...]
    for sweep in range(ITERS - 1):
        coeffs = out_ref[...].astype(BF16)
        own[sweep] = coeffs
        for_east[sweep] = dot_t(east_ref[...], coeffs).astype(BF16)
        send(sweep, 0)
        send(sweep, 1)
        for_south[sweep] = dot_t(south_ref[...], coeffs).astype(BF16)
        send(sweep, 2)
        send(sweep, 3)
        total[...] = jnp.zeros_like(total)
        for side in (1, 3, 0, 2):
            @pl.when(sides[side][0])
            def _():
                arrival(sweep, side).wait_recv()
                value = got[sweep, side]
                if side == 2:
                    total[...] += dot(east_ref[...], value)
                elif side == 3:
                    total[...] += dot(south_ref[...], value)
                else:
                    total[...] += value.astype(F32)

        out_ref[...] = (
            (1.0 - damping) * out_ref[...]
            + first_ref[...]
            - damping * dot(inv_ref[...], total[...].astype(BF16))
        )
    for sweep in range(ITERS - 1):
        for side in range(4):
            @pl.when(sides[side][0])
            def _():
                copy_to(sweep, side).wait_send()


def sweeps_of(n_sx, n_sy, inverse, first, east, south):
    shape = first.shape
    further = ITERS - 1
    return pl.pallas_call(
        functools.partial(sweep_kernel, n_sx, n_sy),
        out_shape=jax.ShapeDtypeStruct(shape, F32),
        in_specs=[VMEM] * 4,
        out_specs=VMEM,
        scratch_shapes=[
            pltpu.VMEM((further,) + shape, BF16),
            pltpu.VMEM((further,) + shape, BF16),
            pltpu.VMEM((further,) + shape, BF16),
            pltpu.VMEM((further, 4) + shape, BF16),
            pltpu.VMEM(shape, F32),
            pltpu.SemaphoreType.DMA((further, 4)),
            pltpu.SemaphoreType.DMA((further, 4)),
        ],
        compiler_params=pltpu.CompilerParams(collective_id=0, has_side_effects=True),
        name="sweeps",
    )(inverse, first, east, south)


def solution(mesh):
    n_sx, n_sy = mesh.shape["sx"], mesh.shape["sy"]

    def on_device(basis, diag_weight, correlation_weight, tile_ids, pair_live, loads, load_count):
        basis = basis[0, 0]
        ids = tile_ids[0, 0]
        row_at, col_at = lax.axis_index("sx"), lax.axis_index("sy")
        live = pair_live[row_at, col_at]
        live_east = jnp.logical_and(live[0] > 0, col_at < n_sy - 1)
        live_south = jnp.logical_and(live[1] > 0, row_at < n_sx - 1)
        lives = jnp.stack([live_east, live_south]).astype(F32)
        loads = loads[0, 0]
        count = (jnp.arange(loads.shape[1])[None, :] < load_count).astype(F32)
        a, x, size, inverse, first, block_east, block_south = assemble(
            n_sx, n_sy, ids, lives, count, basis, correlation_weight[0, 0], diag_weight[0, 0], loads
        )
        inverse, first = finish(count, size, a, x, loads, inverse, first)
        coeffs = sweeps_of(n_sx, n_sy, inverse, first, block_east, block_south)
        return coeffs[None, None]

    return jax.shard_map(
        on_device,
        mesh=mesh,
        in_specs=(
            P("sx", "sy", None, None),
            P("sx", "sy", None),
            P("sx", "sy", None, None),
            P("sx", "sy", None, None),
            P(),
            P("sx", "sy", None, None),
            P("sx", "sy"),
        ),
        out_specs=P("sx", "sy", None, None),
        check_vma=False,
    )
```

```python
import functools

import jax
import jax.numpy as jnp
from jax import lax
from jax.experimental import pallas as pl
from jax.experimental.pallas import tpu as pltpu
from jax.sharding import PartitionSpec as P

TILE = 128
ITERS = 3
HALO = 16
damping = 0.8
MESH = pl.DeviceIdType.MESH
F32 = jnp.float32
BF16 = jnp.bfloat16
VMEM = pl.BlockSpec(memory_space=pltpu.VMEM)
SMEM = pl.BlockSpec(memory_space=pltpu.SMEM)
ANY = pl.BlockSpec(memory_space=pl.ANY)


def dot(a, b):
    return jnp.dot(a, b, preferred_element_type=F32)


def dot_t(a, b):
    return lax.dot_general(a, b, (((0,), (0,)), ((), ())), preferred_element_type=F32)


def split(a):
    high = a.astype(BF16)
    return high, (a - high.astype(F32)).astype(BF16)


def dot3(a, b):
    return dot(a[0], b[0]) + (dot(a[0], b[1]) + dot(a[1], b[0]))


def tile_of(basis_ref, ids_ref, side, t):
    return basis_ref[ids_ref[side, t]]


def image_tile(basis_ref, ids_ref, side, t, tiles, scale):
    width = basis_ref.shape[2]
    scale = jnp.broadcast_to(scale, (TILE, TILE)).T
    scale = jnp.concatenate([scale] * (width // TILE), axis=1)
    before = ids_ref[side, lax.rem(t + tiles - 1, tiles)]
    after = ids_ref[side, lax.rem(t + 1, tiles)]
    first = basis_ref[before, TILE - HALO :, :].astype(F32)
    last = basis_ref[after, :HALO, :].astype(F32)
    first = first * (t > 0).astype(F32)
    last = last * (t < tiles - 1).astype(F32)
    here = tile_of(basis_ref, ids_ref, side, t).astype(F32)
    values = jnp.concatenate([first, here, last], axis=0)
    before = values[HALO - 1 : HALO - 1 + TILE]
    after = values[HALO + 1 : HALO + 1 + TILE]
    return (scale * (2.5 * here - before - after)).astype(BF16)


def eye_like(a):
    row_at = lax.broadcasted_iota(jnp.int32, a.shape, 0)
    col_at = lax.broadcasted_iota(jnp.int32, a.shape, 1)
    return jnp.where(row_at == col_at, 1.0, 0.0).astype(F32)


def norm_bound(a):
    return jnp.max(jnp.sum(jnp.abs(a), axis=0, keepdims=True), axis=1, keepdims=True)


def fine_step(split_a, x):
    split_x = split(x)
    r = eye_like(x) - dot3(split_a, split_x)
    return x + dot3(split_x, split(r)), jnp.sum(r * r, axis=0, keepdims=True)


def first_coeffs(split_a, inverse, loads, carried):
    column = lax.broadcasted_iota(jnp.int32, loads.shape, 1)
    rhs = loads * jnp.clip(carried - column, 0, 1).astype(F32)
    y = dot(inverse, rhs.astype(BF16))
    y = y + dot(inverse, (rhs - dot3(split_a, split(y))).astype(BF16))
    return damping * y


def neighbours(n_sx, n_sy):
    row, col = lax.axis_index("sx"), lax.axis_index("sy")
    west = (col > 0, (row, col - 1))
    north = (row > 0, (row - 1, col))
    east = (col < n_sy - 1, (row, col + 1))
    south = (row < n_sx - 1, (row + 1, col))
    return west, north, east, south


def meet(sides):
    barrier = pltpu.get_barrier_semaphore()
    present = jnp.int32(0)
    for there, place in sides:
        present = present + there.astype(jnp.int32)

        @pl.when(there)
        def _():
            pl.semaphore_signal(barrier, inc=1, device_id=place, device_id_type=MESH)

    pl.semaphore_wait(barrier, present)


def assemble_kernel(
    n_sx, n_sy, ids_ref, live_ref, count_ref, basis_hbm, corr_ref, weight_ref, loads_ref,
    a_out, x_out, size_ref, inv_ref, first_ref, east_ref, south_ref,
    basis_ref, a_ref, x_ref, block_ref, sent, got, send_sem, recv_sem, local_sem,
):
    rows, width = basis_ref.shape[0] * TILE, basis_ref.shape[2]
    half = width // 2
    tiles = corr_ref.shape[1] // TILE
    per = 2 if tiles % 2 == 0 else 1
    chunk = per * TILE
    chunks = tiles // per
    sides = neighbours(n_sx, n_sy)
    parts = 4
    share = basis_ref.shape[0] // parts
    loading = [
        pltpu.make_async_copy(
            basis_hbm.at[pl.ds(k * share, share)],
            basis_ref.at[pl.ds(k * share, share)],
            local_sem.at[2 + k],
        )
        for k in range(parts)
    ]
    for copy in loading:
        copy.start()
    meet(sides)
    for copy in loading:
        copy.wait()

    def piece(which, q, peer):
        at = pl.ds(pl.multiple_of(q * chunk, chunk), chunk)
        return pltpu.make_async_remote_copy(
            src_ref=sent.at[which, at, :],
            dst_ref=got.at[which, at, :],
            send_sem=send_sem.at[which, q],
            recv_sem=recv_sem.at[which, q],
            device_id=sides[peer][1],
            device_id_type=MESH,
        )

    for which in range(2):

        @pl.when(sides[which][0])
        def _():
            @pl.loop(0, chunks)
            def _(q):
                for k in range(per):
                    t = q * per + k
                    at = pl.ds(pl.multiple_of(t * TILE, TILE), TILE)
                    sent[which, at, :] = image_tile(
                        basis_ref, ids_ref, 2 * which, t, tiles, corr_ref[which : which + 1, at]
                    )
                piece(which, q, which).start()

    a_ref[...] = jnp.zeros_like(a_ref)
    step_tiles = 8
    step_rows = step_tiles * TILE

    @pl.loop(0, rows // step_rows)
    def _(i):
        part = basis_ref[pl.ds(i * step_tiles, step_tiles)].reshape(step_rows, width)
        scale = weight_ref[pl.ds(pl.multiple_of(i * step_tiles, step_tiles), step_tiles), :]
        turned = part.T
        pieces = []
        for t in range(step_tiles):
            tile = turned[:, t * TILE : (t + 1) * TILE].astype(F32)
            pieces.append((tile * scale[t : t + 1, :]).astype(BF16))
        weighted = jnp.concatenate(pieces, axis=1)
        a_ref[:half, :] += dot(weighted[:half], part)
        a_ref[half:, half:] += dot(weighted[half:], part[:, half:])

    a_ref[half:, :half] = a_ref[:half, half:].T
    a_copy = pltpu.make_async_copy(a_ref, a_out, local_sem.at[0])
    a_copy.start()
    a = a_ref[...]
    bound = norm_bound(a)
    split_a = split(a)
    low = 0.004
    scale = 2.0 / (1.0 + low)
    alpha = scale / bound
    low = scale * low
    low = low * (2.0 - low)
    scale = 2.0 / (1.0 + low)
    low = scale * low
    x_ref[...] = (scale * alpha) * (2.0 * eye_like(a) - alpha * a)

    def coarse(i, low):
        low = low * (2.0 - low)
        scale = 2.0 / (1.0 + low)
        x = x_ref[...]
        xb = x.astype(BF16)
        t = dot(split_a[0], xb)
        x_ref[...] = scale * (2.0 * x - dot(xb, t.astype(BF16)))
        return low * scale

    lax.fori_loop(0, 5, coarse, jnp.float32(low))

    @pl.loop(0, 2)
    def _(i):
        x, size = fine_step(split_a, x_ref[...])
        x_ref[...] = x
        size_ref[...] = size

    x_copy = pltpu.make_async_copy(x_ref, x_out, local_sem.at[1])
    x_copy.start()
    inverse = x_ref[...].astype(BF16)
    inv_ref[...] = inverse
    first_ref[...] = first_coeffs(split_a, inverse, loads_ref[...], count_ref[0, 0])

    for which, out_ref in ((1, south_ref), (0, east_ref)):
        block_ref[...] = jnp.zeros_like(block_ref)

        @pl.when(sides[which + 2][0])
        def _():
            @pl.loop(0, chunks)
            def _(q):
                piece(which, q, which + 2).wait_recv()
                at = pl.ds(pl.multiple_of(q * chunk, chunk), chunk)
                mine = jnp.concatenate(
                    [
                        tile_of(basis_ref, ids_ref, 2 * which + 1, q * per + k)
                        for k in range(per)
                    ],
                    axis=0,
                )
                block_ref[...] += dot_t(mine, got[which, at, :])

        out_ref[...] = (
            block_ref[...] * live_ref[lax.axis_index("sx"), lax.axis_index("sy"), which].astype(F32)
        ).astype(BF16)

    for which in range(2):

        @pl.when(sides[which][0])
        def _():
            @pl.loop(0, chunks)
            def _(q):
                piece(which, q, which).wait_send()

    a_copy.wait()
    x_copy.wait()


def assemble(n_sx, n_sy, ids, live, count, basis, corr, weight, loads):
    rows, width = basis.shape
    overlap = corr.shape[1]
    tiles = overlap // TILE
    chunks = tiles // 2 if tiles % 2 == 0 else tiles
    square = jax.ShapeDtypeStruct((width, width), F32)
    short = jax.ShapeDtypeStruct((width, width), BF16)
    return pl.pallas_call(
        functools.partial(assemble_kernel, n_sx, n_sy),
        out_shape=(
            square, square, jax.ShapeDtypeStruct((1, width), F32), short,
            jax.ShapeDtypeStruct(loads.shape, F32), short, short,
        ),
        in_specs=[SMEM, SMEM, SMEM, ANY, VMEM, VMEM, VMEM],
        out_specs=(ANY, ANY, VMEM, VMEM, VMEM, VMEM, VMEM),
        scratch_shapes=[
            pltpu.VMEM((rows // TILE, TILE, width), BF16),
            pltpu.VMEM((width, width), F32),
            pltpu.VMEM((width, width), F32),
            pltpu.VMEM((width, width), F32),
            pltpu.VMEM((2, overlap, width), BF16),
            pltpu.VMEM((2, overlap, width), BF16),
            pltpu.SemaphoreType.DMA((2, chunks)),
            pltpu.SemaphoreType.DMA((2, chunks)),
            pltpu.SemaphoreType.DMA((6,)),
        ],
        compiler_params=pltpu.CompilerParams(collective_id=1, has_side_effects=True),
        name="assemble",
    )(
        ids, live, count, basis.reshape(rows // TILE, TILE, width), corr,
        weight.reshape(rows // TILE, TILE), loads,
    )


def finish_kernel(
    count_ref, size_ref, a_hbm, x_hbm, loads_hbm, inv_in, first_in, inv_out, first_out,
    a_ref, x_ref, loads_ref, inv_ref, first_ref, sems,
):
    size = jnp.sum(size_ref[...])

    @pl.when(jnp.logical_not(size < 0.01))
    def _():
        inputs = [
            pltpu.make_async_copy(source, target, sems.at[k])
            for k, (source, target) in enumerate(
                ((a_hbm, a_ref), (x_hbm, x_ref), (loads_hbm, loads_ref))
            )
        ]
        for copy in inputs:
            copy.start()
        for copy in inputs:
            copy.wait()
        a = a_ref[...]
        split_a = split(a)

        @pl.when(jnp.logical_not(size < 1.0))
        def _():
            x_ref[...] = eye_like(a) / norm_bound(a)

        def step(state):
            i, _ = state
            x, size = fine_step(split_a, x_ref[...])
            x_ref[...] = x
            return i + 1, jnp.sum(size)

        lax.while_loop(
            lambda s: jnp.logical_and(s[0] < 48, s[1] >= 0.0001),
            step,
            (jnp.int32(0), jnp.float32(1.0)),
        )
        inverse = x_ref[...].astype(BF16)
        inv_ref[...] = inverse
        first_ref[...] = first_coeffs(split_a, inverse, loads_ref[...], count_ref[0, 0])
        outputs = [
            pltpu.make_async_copy(inv_ref, inv_out, sems.at[3]),
            pltpu.make_async_copy(first_ref, first_out, sems.at[4]),
        ]
        for copy in outputs:
            copy.start()
        for copy in outputs:
            copy.wait()


def finish(count, size, a, x, loads, inverse, first):
    square = pltpu.VMEM(a.shape, F32)
    return pl.pallas_call(
        finish_kernel,
        out_shape=(
            jax.ShapeDtypeStruct(inverse.shape, BF16), jax.ShapeDtypeStruct(first.shape, F32),
        ),
        in_specs=[SMEM, VMEM, ANY, ANY, ANY, ANY, ANY],
        out_specs=(ANY, ANY),
        scratch_shapes=[
            square, square, pltpu.VMEM(loads.shape, F32), pltpu.VMEM(inverse.shape, BF16),
            pltpu.VMEM(first.shape, F32), pltpu.SemaphoreType.DMA((5,)),
        ],
        input_output_aliases={5: 0, 6: 1},
        name="finish",
    )(count, size, a, x, loads, inverse, first)


def sweep_kernel(
    n_sx, n_sy, inv_ref, first_ref, east_ref, south_ref, out_ref, own, for_east, for_south,
    got, total, send_sem, recv_sem,
):
    sides = neighbours(n_sx, n_sy)
    meet(sides)

    halves, span = own.shape[1], own.shape[3]

    def copy_to(sweep, part, side):
        source = (own, own, for_east, for_south)[side]
        return pltpu.make_async_remote_copy(
            src_ref=source.at[sweep, part],
            dst_ref=got.at[sweep, part, (side + 2) % 4],
            send_sem=send_sem.at[sweep, part, side],
            recv_sem=recv_sem.at[sweep, part, (side + 2) % 4],
            device_id=sides[side][1],
            device_id_type=MESH,
        )

    def arrival(sweep, part, side):
        place = got.at[sweep, part, side]
        return pltpu.make_async_remote_copy(
            src_ref=place,
            dst_ref=place,
            send_sem=send_sem.at[sweep, part, side],
            recv_sem=recv_sem.at[sweep, part, side],
            device_id=sides[side][1],
            device_id_type=MESH,
        )

    def send(sweep, part, side):
        @pl.when(sides[side][0])
        def _():
            copy_to(sweep, part, side).start()

    def give(sweep, part, coeffs):
        own[sweep, part] = coeffs
        for_east[sweep, part] = dot_t(east_ref[...], coeffs).astype(BF16)
        send(sweep, part, 0)
        send(sweep, part, 1)
        for_south[sweep, part] = dot_t(south_ref[...], coeffs).astype(BF16)
        send(sweep, part, 2)
        send(sweep, part, 3)

    def take(sweep, part, coeffs, initial):
        total[...] = jnp.zeros_like(total)
        for side in (1, 3, 0, 2):
            @pl.when(sides[side][0])
            def _():
                arrival(sweep, part, side).wait_recv()
                value = got[sweep, part, side]
                if side == 2:
                    total[...] += dot(east_ref[...], value)
                elif side == 3:
                    total[...] += dot(south_ref[...], value)
                else:
                    total[...] += value.astype(F32)

        moved = dot(inv_ref[...], total[...].astype(BF16))
        return (1.0 - damping) * coeffs + initial - damping * moved

    for part in range(halves):
        give(0, part, first_ref[:, part * span : (part + 1) * span].astype(BF16))
    for sweep in range(ITERS - 1):
        for part in range(halves):
            at = slice(part * span, (part + 1) * span)
            before = first_ref[:, at] if sweep == 0 else out_ref[:, at]
            coeffs = take(sweep, part, before, first_ref[:, at])
            out_ref[:, at] = coeffs
            if sweep < ITERS - 2:
                give(sweep + 1, part, coeffs.astype(BF16))
    for sweep in range(ITERS - 1):
        for part in range(halves):
            for side in range(4):
                @pl.when(sides[side][0])
                def _():
                    copy_to(sweep, part, side).wait_send()


def sweeps_of(n_sx, n_sy, inverse, first, east, south):
    shape = first.shape
    further = ITERS - 1
    halves = 2 if shape[1] % (2 * TILE) == 0 else 1
    piece = (shape[0], shape[1] // halves)
    return pl.pallas_call(
        functools.partial(sweep_kernel, n_sx, n_sy),
        out_shape=jax.ShapeDtypeStruct(shape, F32),
        in_specs=[VMEM] * 4,
        out_specs=VMEM,
        scratch_shapes=[
            pltpu.VMEM((further, halves) + piece, BF16),
            pltpu.VMEM((further, halves) + piece, BF16),
            pltpu.VMEM((further, halves) + piece, BF16),
            pltpu.VMEM((further, halves, 4) + piece, BF16),
            pltpu.VMEM(piece, F32),
            pltpu.SemaphoreType.DMA((further, halves, 4)),
            pltpu.SemaphoreType.DMA((further, halves, 4)),
        ],
        compiler_params=pltpu.CompilerParams(collective_id=0, has_side_effects=True),
        name="sweeps",
    )(inverse, first, east, south)


def solution(mesh):
    n_sx, n_sy = mesh.shape["sx"], mesh.shape["sy"]

    def on_device(basis, diag_weight, correlation_weight, tile_ids, pair_live, loads, load_count):
        basis = basis[0, 0]
        ids = tile_ids[0, 0]
        loads = loads[0, 0]
        a, x, size, inverse, first, block_east, block_south = assemble(
            n_sx, n_sy, ids, pair_live, load_count, basis, correlation_weight[0, 0], diag_weight[0, 0], loads
        )
        inverse, first = finish(load_count, size, a, x, loads, inverse, first)
        coeffs = sweeps_of(n_sx, n_sy, inverse, first, block_east, block_south)
        return coeffs[None, None]

    return jax.shard_map(
        on_device,
        mesh=mesh,
        in_specs=(
            P("sx", "sy", None, None),
            P("sx", "sy", None),
            P("sx", "sy", None, None),
            P("sx", "sy", None, None),
            P(),
            P("sx", "sy", None, None),
            P("sx", "sy"),
        ),
        out_specs=P("sx", "sy", None, None),
        check_vma=False,
    )
```

```python
import functools

import jax
import jax.numpy as jnp
from jax import lax
from jax.experimental import pallas as pl
from jax.experimental.pallas import tpu as pltpu
from jax.sharding import PartitionSpec as P

TILE = 128
ITERS = 3
HALO = 16
damping = 0.8
MESH = pl.DeviceIdType.MESH
F32 = jnp.float32
BF16 = jnp.bfloat16
VMEM = pl.BlockSpec(memory_space=pltpu.VMEM)
SMEM = pl.BlockSpec(memory_space=pltpu.SMEM)
ANY = pl.BlockSpec(memory_space=pl.ANY)


def dot(a, b):
    return jnp.dot(a, b, preferred_element_type=F32)


def dot_t(a, b):
    return lax.dot_general(a, b, (((0,), (0,)), ((), ())), preferred_element_type=F32)


def split(a):
    high = a.astype(BF16)
    return high, (a - high.astype(F32)).astype(BF16)


def dot3(a, b):
    return dot(a[0], b[0]) + (dot(a[0], b[1]) + dot(a[1], b[0]))


def tile_of(basis_ref, ids_ref, side, t):
    return basis_ref[ids_ref[side, t]]


def image_tile(basis_ref, ids_ref, side, t, tiles, scale):
    width = basis_ref.shape[2]
    scale = jnp.broadcast_to(scale, (TILE, TILE)).T
    scale = jnp.concatenate([scale] * (width // TILE), axis=1)
    before = ids_ref[side, lax.rem(t + tiles - 1, tiles)]
    after = ids_ref[side, lax.rem(t + 1, tiles)]
    first = basis_ref[before, TILE - HALO :, :].astype(F32)
    last = basis_ref[after, :HALO, :].astype(F32)
    first = first * (t > 0).astype(F32)
    last = last * (t < tiles - 1).astype(F32)
    here = tile_of(basis_ref, ids_ref, side, t).astype(F32)
    values = jnp.concatenate([first, here, last], axis=0)
    before = values[HALO - 1 : HALO - 1 + TILE]
    after = values[HALO + 1 : HALO + 1 + TILE]
    return (scale * (2.5 * here - before - after)).astype(BF16)


def eye_like(a):
    row_at = lax.broadcasted_iota(jnp.int32, a.shape, 0)
    col_at = lax.broadcasted_iota(jnp.int32, a.shape, 1)
    return jnp.where(row_at == col_at, 1.0, 0.0).astype(F32)


def norm_bound(a):
    return jnp.max(jnp.sum(jnp.abs(a), axis=0, keepdims=True), axis=1, keepdims=True)


def fine_step(split_a, x):
    split_x = split(x)
    r = eye_like(x) - dot3(split_a, split_x)
    return x + dot3(split_x, split(r)), jnp.sum(r * r, axis=0, keepdims=True)


def first_coeffs(split_a, inverse, loads, carried):
    column = lax.broadcasted_iota(jnp.int32, loads.shape, 1)
    rhs = loads * jnp.clip(carried - column, 0, 1).astype(F32)
    y = dot(inverse, rhs.astype(BF16))
    y = y + dot(inverse, (rhs - dot3(split_a, split(y))).astype(BF16))
    return damping * y


def neighbours(n_sx, n_sy):
    row, col = lax.axis_index("sx"), lax.axis_index("sy")
    west = (col > 0, (row, col - 1))
    north = (row > 0, (row - 1, col))
    east = (col < n_sy - 1, (row, col + 1))
    south = (row < n_sx - 1, (row + 1, col))
    return west, north, east, south


def meet(sides):
    barrier = pltpu.get_barrier_semaphore()
    present = jnp.int32(0)
    for there, place in sides:
        present = present + there.astype(jnp.int32)

        @pl.when(there)
        def _():
            pl.semaphore_signal(barrier, inc=1, device_id=place, device_id_type=MESH)

    pl.semaphore_wait(barrier, present)


def assemble_kernel(
    n_sx, n_sy, ids_ref, live_ref, count_ref, basis_hbm, corr_ref, weight_ref, loads_ref,
    a_out, x_out, size_ref, inv_ref, first_ref, east_ref, south_ref,
    basis_ref, a_ref, x_ref, block_ref, sent, got, send_sem, recv_sem, local_sem,
):
    rows, width = basis_ref.shape[0] * TILE, basis_ref.shape[2]
    half = width // 2
    tiles = corr_ref.shape[1] // TILE
    per = 2 if tiles % 2 == 0 else 1
    chunk = per * TILE
    chunks = tiles // per
    sides = neighbours(n_sx, n_sy)
    parts = 4
    share = basis_ref.shape[0] // parts
    loading = [
        pltpu.make_async_copy(
            basis_hbm.at[pl.ds(k * share, share)],
            basis_ref.at[pl.ds(k * share, share)],
            local_sem.at[2 + k],
        )
        for k in range(parts)
    ]
    for copy in loading:
        copy.start()
    meet(sides)
    for copy in loading:
        copy.wait()

    def piece(which, q, peer):
        at = pl.ds(pl.multiple_of(q * chunk, chunk), chunk)
        return pltpu.make_async_remote_copy(
            src_ref=sent.at[which, at, :],
            dst_ref=got.at[which, at, :],
            send_sem=send_sem.at[which, q],
            recv_sem=recv_sem.at[which, q],
            device_id=sides[peer][1],
            device_id_type=MESH,
        )

    for which in range(2):

        @pl.when(sides[which][0])
        def _():
            @pl.loop(0, chunks)
            def _(q):
                for k in range(per):
                    t = q * per + k
                    at = pl.ds(pl.multiple_of(t * TILE, TILE), TILE)
                    sent[which, at, :] = image_tile(
                        basis_ref, ids_ref, 2 * which, t, tiles, corr_ref[which : which + 1, at]
                    )
                piece(which, q, which).start()

    a_ref[...] = jnp.zeros_like(a_ref)
    step_tiles = 8
    step_rows = step_tiles * TILE

    @pl.loop(0, rows // step_rows)
    def _(i):
        part = basis_ref[pl.ds(i * step_tiles, step_tiles)].reshape(step_rows, width)
        scale = weight_ref[pl.ds(pl.multiple_of(i * step_tiles, step_tiles), step_tiles), :]
        turned = part.T
        pieces = []
        for t in range(step_tiles):
            tile = turned[:, t * TILE : (t + 1) * TILE].astype(F32)
            pieces.append((tile * scale[t : t + 1, :]).astype(BF16))
        weighted = jnp.concatenate(pieces, axis=1)
        a_ref[:half, :] += dot(weighted[:half], part)
        a_ref[half:, half:] += dot(weighted[half:], part[:, half:])

    a_ref[half:, :half] = a_ref[:half, half:].T
    a_copy = pltpu.make_async_copy(a_ref, a_out, local_sem.at[0])
    a_copy.start()
    a = a_ref[...]
    bound = norm_bound(a)
    split_a = split(a)
    low = 0.004
    scale = 2.0 / (1.0 + low)
    alpha = scale / bound
    low = scale * low
    low = low * (2.0 - low)
    scale = 2.0 / (1.0 + low)
    low = scale * low
    x_ref[...] = (scale * alpha) * (2.0 * eye_like(a) - alpha * a)

    def coarse(i, low):
        low = low * (2.0 - low)
        scale = 2.0 / (1.0 + low)
        x = x_ref[...]
        xb = x.astype(BF16)
        t = dot(split_a[0], xb)
        x_ref[...] = scale * (2.0 * x - dot(xb, t.astype(BF16)))
        return low * scale

    lax.fori_loop(0, 5, coarse, jnp.float32(low))

    @pl.loop(0, 2)
    def _(i):
        x, size = fine_step(split_a, x_ref[...])
        x_ref[...] = x
        size_ref[...] = size

    x_copy = pltpu.make_async_copy(x_ref, x_out, local_sem.at[1])
    x_copy.start()
    inverse = x_ref[...].astype(BF16)
    inv_ref[...] = inverse
    first_ref[...] = first_coeffs(split_a, inverse, loads_ref[...], count_ref[0, 0])

    for which, out_ref in ((1, south_ref), (0, east_ref)):
        block_ref[...] = jnp.zeros_like(block_ref)

        @pl.when(sides[which + 2][0])
        def _():
            @pl.loop(0, chunks)
            def _(q):
                piece(which, q, which + 2).wait_recv()
                at = pl.ds(pl.multiple_of(q * chunk, chunk), chunk)
                mine = jnp.concatenate(
                    [
                        tile_of(basis_ref, ids_ref, 2 * which + 1, q * per + k)
                        for k in range(per)
                    ],
                    axis=0,
                )
                there = got[which, at, :]
                block_ref[0] += dot_t(mine, there)
                block_ref[1] += dot_t(there, mine)

        live = live_ref[lax.axis_index("sx"), which, lax.axis_index("sy")].astype(F32)
        for k in range(2):
            out_ref[k] = (block_ref[k] * live).astype(BF16)

    for which in range(2):

        @pl.when(sides[which][0])
        def _():
            @pl.loop(0, chunks)
            def _(q):
                piece(which, q, which).wait_send()

    a_copy.wait()
    x_copy.wait()


def assemble(n_sx, n_sy, ids, live, count, basis, corr, weight, loads):
    rows, width = basis.shape
    overlap = corr.shape[1]
    tiles = overlap // TILE
    chunks = tiles // 2 if tiles % 2 == 0 else tiles
    square = jax.ShapeDtypeStruct((width, width), F32)
    short = jax.ShapeDtypeStruct((width, width), BF16)
    pair = jax.ShapeDtypeStruct((2, width, width), BF16)
    return pl.pallas_call(
        functools.partial(assemble_kernel, n_sx, n_sy),
        out_shape=(
            square, square, jax.ShapeDtypeStruct((1, width), F32), short,
            jax.ShapeDtypeStruct(loads.shape, F32), pair, pair,
        ),
        in_specs=[SMEM, SMEM, SMEM, ANY, VMEM, VMEM, VMEM],
        out_specs=(ANY, ANY, VMEM, VMEM, VMEM, VMEM, VMEM),
        scratch_shapes=[
            pltpu.VMEM((rows // TILE, TILE, width), BF16),
            pltpu.VMEM((width, width), F32),
            pltpu.VMEM((width, width), F32),
            pltpu.VMEM((2, width, width), F32),
            pltpu.VMEM((2, overlap, width), BF16),
            pltpu.VMEM((2, overlap, width), BF16),
            pltpu.SemaphoreType.DMA((2, chunks)),
            pltpu.SemaphoreType.DMA((2, chunks)),
            pltpu.SemaphoreType.DMA((6,)),
        ],
        compiler_params=pltpu.CompilerParams(collective_id=1, has_side_effects=True),
        name="assemble",
    )(
        ids, live, count, basis.reshape(rows // TILE, TILE, width), corr,
        weight.reshape(rows // TILE, TILE), loads,
    )


def finish_kernel(
    count_ref, size_ref, a_hbm, x_hbm, loads_hbm, inv_in, first_in, inv_out, first_out,
    a_ref, x_ref, loads_ref, inv_ref, first_ref, sems,
):
    size = jnp.sum(size_ref[...])

    @pl.when(jnp.logical_not(size < 0.01))
    def _():
        inputs = [
            pltpu.make_async_copy(source, target, sems.at[k])
            for k, (source, target) in enumerate(
                ((a_hbm, a_ref), (x_hbm, x_ref), (loads_hbm, loads_ref))
            )
        ]
        for copy in inputs:
            copy.start()
        for copy in inputs:
            copy.wait()
        a = a_ref[...]
        split_a = split(a)

        @pl.when(jnp.logical_not(size < 1.0))
        def _():
            x_ref[...] = eye_like(a) / norm_bound(a)

        def step(state):
            i, _ = state
            x, size = fine_step(split_a, x_ref[...])
            x_ref[...] = x
            return i + 1, jnp.sum(size)

        lax.while_loop(
            lambda s: jnp.logical_and(s[0] < 48, s[1] >= 0.0001),
            step,
            (jnp.int32(0), jnp.float32(1.0)),
        )
        inverse = x_ref[...].astype(BF16)
        inv_ref[...] = inverse
        first_ref[...] = first_coeffs(split_a, inverse, loads_ref[...], count_ref[0, 0])
        outputs = [
            pltpu.make_async_copy(inv_ref, inv_out, sems.at[3]),
            pltpu.make_async_copy(first_ref, first_out, sems.at[4]),
        ]
        for copy in outputs:
            copy.start()
        for copy in outputs:
            copy.wait()


def finish(count, size, a, x, loads, inverse, first):
    square = pltpu.VMEM(a.shape, F32)
    return pl.pallas_call(
        finish_kernel,
        out_shape=(
            jax.ShapeDtypeStruct(inverse.shape, BF16), jax.ShapeDtypeStruct(first.shape, F32),
        ),
        in_specs=[SMEM, VMEM, ANY, ANY, ANY, ANY, ANY],
        out_specs=(ANY, ANY),
        scratch_shapes=[
            square, square, pltpu.VMEM(loads.shape, F32), pltpu.VMEM(inverse.shape, BF16),
            pltpu.VMEM(first.shape, F32), pltpu.SemaphoreType.DMA((5,)),
        ],
        input_output_aliases={5: 0, 6: 1},
        name="finish",
    )(count, size, a, x, loads, inverse, first)


def sweep_kernel(
    n_sx, n_sy, inv_ref, first_ref, east_ref, south_ref, out_ref, rest_ref, own, for_east, for_south,
    got, total, send_sem, recv_sem,
):
    sides = neighbours(n_sx, n_sy)
    meet(sides)

    halves, span = own.shape[1], own.shape[3]

    def copy_to(sweep, part, side):
        source = (own, own, for_east, for_south)[side]
        return pltpu.make_async_remote_copy(
            src_ref=source.at[sweep, part],
            dst_ref=got.at[sweep, part, (side + 2) % 4],
            send_sem=send_sem.at[sweep, part, side],
            recv_sem=recv_sem.at[sweep, part, (side + 2) % 4],
            device_id=sides[side][1],
            device_id_type=MESH,
        )

    def arrival(sweep, part, side):
        place = got.at[sweep, part, side]
        return pltpu.make_async_remote_copy(
            src_ref=place,
            dst_ref=place,
            send_sem=send_sem.at[sweep, part, side],
            recv_sem=recv_sem.at[sweep, part, side],
            device_id=sides[side][1],
            device_id_type=MESH,
        )

    def send(sweep, part, side):
        @pl.when(sides[side][0])
        def _():
            copy_to(sweep, part, side).start()

    def give_own(sweep, part, coeffs):
        own[sweep, part] = coeffs
        send(sweep, part, 0)
        send(sweep, part, 1)

    def give_products(sweep, part, coeffs):
        for_east[sweep, part] = dot(east_ref[1], coeffs).astype(BF16)
        for_south[sweep, part] = dot(south_ref[1], coeffs).astype(BF16)
        send(sweep, part, 2)
        send(sweep, part, 3)

    def take(sweep, part):
        total[...] = jnp.zeros_like(total)
        for side in (1, 3, 0, 2):
            @pl.when(sides[side][0])
            def _():
                arrival(sweep, part, side).wait_recv()
                value = got[sweep, part, side]
                if side == 2:
                    total[...] += dot(east_ref[0], value)
                elif side == 3:
                    total[...] += dot(south_ref[0], value)
                else:
                    total[...] += value.astype(F32)

    spans = [slice(part * span, (part + 1) * span) for part in range(halves)]
    coeffs = [first_ref[:, at].astype(BF16) for at in spans]
    for part in range(halves):
        give_own(0, part, coeffs[part])
    for part in range(halves):
        give_products(0, part, coeffs[part])
    out_ref[...] = (2.0 - damping) * first_ref[...]
    for sweep in range(ITERS - 1):
        for part, at in enumerate(spans):
            take(sweep, part)
            if sweep == ITERS - 2:
                rest_ref[:, at] = total[...].astype(BF16)
                continue
            moved = out_ref[:, at] - damping * dot(inv_ref[...], total[...].astype(BF16))
            coeffs = moved.astype(BF16)
            give_own(sweep + 1, part, coeffs)
            give_products(sweep + 1, part, coeffs)
            out_ref[:, at] = (1.0 - damping) * moved + first_ref[:, at]
    for sweep in range(ITERS - 1):
        for part in range(halves):
            for side in range(4):
                @pl.when(sides[side][0])
                def _():
                    copy_to(sweep, part, side).wait_send()


def settle_kernel(inv_ref, part_ref, rest_ref, out_ref):
    out_ref[...] = part_ref[...] - damping * dot(inv_ref[...], rest_ref[...])


def settle(inverse, part, rest):
    return pl.pallas_call(
        settle_kernel,
        out_shape=jax.ShapeDtypeStruct(part.shape, F32),
        in_specs=[VMEM] * 3,
        out_specs=VMEM,
        name="settle",
    )(inverse, part, rest)


def sweeps_of(n_sx, n_sy, inverse, first, east, south):
    shape = first.shape
    further = ITERS - 1
    halves = 2 if shape[1] % (2 * TILE) == 0 else 1
    piece = (shape[0], shape[1] // halves)
    return pl.pallas_call(
        functools.partial(sweep_kernel, n_sx, n_sy),
        out_shape=(jax.ShapeDtypeStruct(shape, F32), jax.ShapeDtypeStruct(shape, BF16)),
        in_specs=[VMEM] * 4,
        out_specs=(VMEM, VMEM),
        scratch_shapes=[
            pltpu.VMEM((further, halves) + piece, BF16),
            pltpu.VMEM((further, halves) + piece, BF16),
            pltpu.VMEM((further, halves) + piece, BF16),
            pltpu.VMEM((further, halves, 4) + piece, BF16),
            pltpu.VMEM(piece, F32),
            pltpu.SemaphoreType.DMA((further, halves, 4)),
            pltpu.SemaphoreType.DMA((further, halves, 4)),
        ],
        compiler_params=pltpu.CompilerParams(collective_id=0, has_side_effects=True),
        name="sweeps",
    )(inverse, first, east, south)


def solution(mesh):
    n_sx, n_sy = mesh.shape["sx"], mesh.shape["sy"]

    def on_device(basis, diag_weight, correlation_weight, tile_ids, pair_live, loads, load_count):
        basis = basis[0, 0]
        ids = tile_ids[0, 0]
        loads = loads[0, 0]
        a, x, size, inverse, first, block_east, block_south = assemble(
            n_sx, n_sy, ids, pair_live.transpose(0, 2, 1), load_count, basis, correlation_weight[0, 0], diag_weight[0, 0], loads
        )
        inverse, first = finish(load_count, size, a, x, loads, inverse, first)
        part, rest = sweeps_of(n_sx, n_sy, inverse, first, block_east, block_south)
        coeffs = settle(inverse, part, rest)
        return coeffs[None, None]

    return jax.shard_map(
        on_device,
        mesh=mesh,
        in_specs=(
            P("sx", "sy", None, None),
            P("sx", "sy", None),
            P("sx", "sy", None, None),
            P("sx", "sy", None, None),
            P(),
            P("sx", "sy", None, None),
            P("sx", "sy"),
        ),
        out_specs=P("sx", "sy", None, None),
        check_vma=False,
    )
```

```python
import functools

import jax
import jax.numpy as jnp
from jax import lax
from jax.experimental import pallas as pl
from jax.experimental.pallas import tpu as pltpu
from jax.sharding import PartitionSpec as P

TILE = 128
ITERS = 3
HALO = 16
damping = 0.8
MESH = pl.DeviceIdType.MESH
F32 = jnp.float32
BF16 = jnp.bfloat16
VMEM = pl.BlockSpec(memory_space=pltpu.VMEM)
SMEM = pl.BlockSpec(memory_space=pltpu.SMEM)
ANY = pl.BlockSpec(memory_space=pl.ANY)


def dot(a, b):
    return jnp.dot(a, b, preferred_element_type=F32)


def dot_t(a, b):
    return lax.dot_general(a, b, (((0,), (0,)), ((), ())), preferred_element_type=F32)


def split(a):
    high = a.astype(BF16)
    return high, (a - high.astype(F32)).astype(BF16)


def dot3(a, b):
    return dot(a[0], b[0]) + (dot(a[0], b[1]) + dot(a[1], b[0]))


def tile_of(basis_ref, ids_ref, side, t):
    return basis_ref[ids_ref[side, t]]


def image_tile(basis_ref, ids_ref, side, t, tiles, scale):
    width = basis_ref.shape[2]
    scale = jnp.broadcast_to(scale, (TILE, TILE)).T
    scale = jnp.concatenate([scale] * (width // TILE), axis=1)
    before = ids_ref[side, lax.rem(t + tiles - 1, tiles)]
    after = ids_ref[side, lax.rem(t + 1, tiles)]
    first = basis_ref[before, TILE - HALO :, :].astype(F32)
    last = basis_ref[after, :HALO, :].astype(F32)
    first = first * (t > 0).astype(F32)
    last = last * (t < tiles - 1).astype(F32)
    here = tile_of(basis_ref, ids_ref, side, t).astype(F32)
    values = jnp.concatenate([first, here, last], axis=0)
    before = values[HALO - 1 : HALO - 1 + TILE]
    after = values[HALO + 1 : HALO + 1 + TILE]
    return (scale * (2.5 * here - before - after)).astype(BF16)


def eye_like(a):
    row_at = lax.broadcasted_iota(jnp.int32, a.shape, 0)
    col_at = lax.broadcasted_iota(jnp.int32, a.shape, 1)
    return jnp.where(row_at == col_at, 1.0, 0.0).astype(F32)


def norm_bound(a):
    return jnp.max(jnp.sum(jnp.abs(a), axis=0, keepdims=True), axis=1, keepdims=True)


def fine_step(split_a, x):
    split_x = split(x)
    r = eye_like(x) - dot3(split_a, split_x)
    return x + dot3(split_x, split(r)), jnp.sum(r * r, axis=0, keepdims=True)


def first_coeffs(split_a, inverse, loads, carried):
    column = lax.broadcasted_iota(jnp.int32, loads.shape, 1)
    rhs = loads * jnp.clip(carried - column, 0, 1).astype(F32)
    y = dot(inverse, rhs.astype(BF16))
    y = y + dot(inverse, (rhs - dot3(split_a, split(y))).astype(BF16))
    return damping * y


def neighbours(n_sx, n_sy):
    row, col = lax.axis_index("sx"), lax.axis_index("sy")
    west = (col > 0, (row, col - 1))
    north = (row > 0, (row - 1, col))
    east = (col < n_sy - 1, (row, col + 1))
    south = (row < n_sx - 1, (row + 1, col))
    return west, north, east, south


def meet(sides):
    barrier = pltpu.get_barrier_semaphore()
    present = jnp.int32(0)
    for there, place in sides:
        present = present + there.astype(jnp.int32)

        @pl.when(there)
        def _():
            pl.semaphore_signal(barrier, inc=1, device_id=place, device_id_type=MESH)

    pl.semaphore_wait(barrier, present)


def assemble_kernel(
    n_sx, n_sy, ids_ref, live_ref, count_ref, basis_hbm, corr_ref, weight_ref, loads_ref,
    a_out, x_out, size_ref, inv_ref, first_ref, east_ref, south_ref,
    basis_ref, a_ref, x_ref, block_ref, sent, got, send_sem, recv_sem, local_sem,
):
    rows, width = basis_ref.shape[0] * TILE, basis_ref.shape[2]
    half = width // 2
    tiles = corr_ref.shape[1] // TILE
    per = 2 if tiles % 2 == 0 else 1
    chunk = per * TILE
    chunks = tiles // per
    sides = neighbours(n_sx, n_sy)
    parts = 4
    share = basis_ref.shape[0] // parts
    loading = [
        pltpu.make_async_copy(
            basis_hbm.at[pl.ds(k * share, share)],
            basis_ref.at[pl.ds(k * share, share)],
            local_sem.at[2 + k],
        )
        for k in range(parts)
    ]
    for copy in loading:
        copy.start()
    meet(sides)
    for copy in loading:
        copy.wait()

    def piece(which, q, peer):
        at = pl.ds(pl.multiple_of(q * chunk, chunk), chunk)
        return pltpu.make_async_remote_copy(
            src_ref=sent.at[which, at, :],
            dst_ref=got.at[which, at, :],
            send_sem=send_sem.at[which, q],
            recv_sem=recv_sem.at[which, q],
            device_id=sides[peer][1],
            device_id_type=MESH,
        )

    for which in range(2):

        @pl.when(sides[which][0])
        def _():
            @pl.loop(0, chunks)
            def _(q):
                for k in range(per):
                    t = q * per + k
                    at = pl.ds(pl.multiple_of(t * TILE, TILE), TILE)
                    sent[which, at, :] = image_tile(
                        basis_ref, ids_ref, 2 * which, t, tiles, corr_ref[which : which + 1, at]
                    )
                piece(which, q, which).start()

    a_ref[...] = jnp.zeros_like(a_ref)
    step_tiles = 8
    step_rows = step_tiles * TILE

    @pl.loop(0, rows // step_rows)
    def _(i):
        part = basis_ref[pl.ds(i * step_tiles, step_tiles)].reshape(step_rows, width)
        scale = weight_ref[pl.ds(pl.multiple_of(i * step_tiles, step_tiles), step_tiles), :]
        turned = part.T
        pieces = []
        for t in range(step_tiles):
            tile = turned[:, t * TILE : (t + 1) * TILE].astype(F32)
            pieces.append((tile * scale[t : t + 1, :]).astype(BF16))
        weighted = jnp.concatenate(pieces, axis=1)
        a_ref[:half, :] += dot(weighted[:half], part)
        a_ref[half:, half:] += dot(weighted[half:], part[:, half:])

    a_ref[half:, :half] = a_ref[:half, half:].T
    a_copy = pltpu.make_async_copy(a_ref, a_out, local_sem.at[0])
    a_copy.start()
    a = a_ref[...]
    bound = norm_bound(a)
    split_a = split(a)
    low = 0.004
    scale = 2.0 / (1.0 + low)
    alpha = scale / bound
    low = scale * low
    low = low * (2.0 - low)
    scale = 2.0 / (1.0 + low)
    low = scale * low
    x_ref[...] = (scale * alpha) * (2.0 * eye_like(a) - alpha * a)

    def coarse(i, low):
        low = low * (2.0 - low)
        scale = 2.0 / (1.0 + low)
        x = x_ref[...]
        xb = x.astype(BF16)
        t = dot(split_a[0], xb)
        x_ref[...] = scale * (2.0 * x - dot(xb, t.astype(BF16)))
        return low * scale

    lax.fori_loop(0, 5, coarse, jnp.float32(low))

    @pl.loop(0, 2)
    def _(i):
        x, size = fine_step(split_a, x_ref[...])
        x_ref[...] = x
        size_ref[...] = size

    x_copy = pltpu.make_async_copy(x_ref, x_out, local_sem.at[1])
    x_copy.start()
    inverse = x_ref[...].astype(BF16)
    inv_ref[...] = inverse
    first_ref[...] = first_coeffs(split_a, inverse, loads_ref[...], count_ref[0, 0])

    for which, out_ref in ((1, south_ref), (0, east_ref)):
        block_ref[...] = jnp.zeros_like(block_ref)

        @pl.when(sides[which + 2][0])
        def _():
            @pl.loop(0, chunks)
            def _(q):
                piece(which, q, which + 2).wait_recv()
                at = pl.ds(pl.multiple_of(q * chunk, chunk), chunk)
                mine = jnp.concatenate(
                    [
                        tile_of(basis_ref, ids_ref, 2 * which + 1, q * per + k)
                        for k in range(per)
                    ],
                    axis=0,
                )
                there = got[which, at, :]
                block_ref[0] += dot_t(mine, there)
                block_ref[1] += dot_t(there, mine)

        live = live_ref[lax.axis_index("sx"), which, lax.axis_index("sy")].astype(F32)
        for k in range(2):
            out_ref[k] = (block_ref[k] * live).astype(BF16)

    for which in range(2):

        @pl.when(sides[which][0])
        def _():
            @pl.loop(0, chunks)
            def _(q):
                piece(which, q, which).wait_send()

    a_copy.wait()
    x_copy.wait()


def assemble(n_sx, n_sy, ids, live, count, basis, corr, weight, loads):
    rows, width = basis.shape
    overlap = corr.shape[1]
    tiles = overlap // TILE
    chunks = tiles // 2 if tiles % 2 == 0 else tiles
    square = jax.ShapeDtypeStruct((width, width), F32)
    short = jax.ShapeDtypeStruct((width, width), BF16)
    pair = jax.ShapeDtypeStruct((2, width, width), BF16)
    return pl.pallas_call(
        functools.partial(assemble_kernel, n_sx, n_sy),
        out_shape=(
            square, square, jax.ShapeDtypeStruct((1, width), F32), short,
            jax.ShapeDtypeStruct(loads.shape, F32), pair, pair,
        ),
        in_specs=[SMEM, SMEM, SMEM, ANY, VMEM, VMEM, VMEM],
        out_specs=(ANY, ANY, VMEM, VMEM, VMEM, VMEM, VMEM),
        scratch_shapes=[
            pltpu.VMEM((rows // TILE, TILE, width), BF16),
            pltpu.VMEM((width, width), F32),
            pltpu.VMEM((width, width), F32),
            pltpu.VMEM((2, width, width), F32),
            pltpu.VMEM((2, overlap, width), BF16),
            pltpu.VMEM((2, overlap, width), BF16),
            pltpu.SemaphoreType.DMA((2, chunks)),
            pltpu.SemaphoreType.DMA((2, chunks)),
            pltpu.SemaphoreType.DMA((6,)),
        ],
        compiler_params=pltpu.CompilerParams(collective_id=1, has_side_effects=True),
        name="assemble",
    )(
        ids, live, count, basis.reshape(rows // TILE, TILE, width), corr,
        weight.reshape(rows // TILE, TILE), loads,
    )


def finish_kernel(
    count_ref, size_ref, a_hbm, x_hbm, loads_hbm, inv_in, first_in, inv_out, first_out,
    a_ref, x_ref, loads_ref, inv_ref, first_ref, sems,
):
    size = jnp.sum(size_ref[...])

    @pl.when(jnp.logical_not(size < 0.01))
    def _():
        inputs = [
            pltpu.make_async_copy(source, target, sems.at[k])
            for k, (source, target) in enumerate(
                ((a_hbm, a_ref), (x_hbm, x_ref), (loads_hbm, loads_ref))
            )
        ]
        for copy in inputs:
            copy.start()
        for copy in inputs:
            copy.wait()
        a = a_ref[...]
        split_a = split(a)

        @pl.when(jnp.logical_not(size < 1.0))
        def _():
            x_ref[...] = eye_like(a) / norm_bound(a)

        def step(state):
            i, _ = state
            x, size = fine_step(split_a, x_ref[...])
            x_ref[...] = x
            return i + 1, jnp.sum(size)

        lax.while_loop(
            lambda s: jnp.logical_and(s[0] < 48, s[1] >= 0.0001),
            step,
            (jnp.int32(0), jnp.float32(1.0)),
        )
        inverse = x_ref[...].astype(BF16)
        inv_ref[...] = inverse
        first_ref[...] = first_coeffs(split_a, inverse, loads_ref[...], count_ref[0, 0])
        outputs = [
            pltpu.make_async_copy(inv_ref, inv_out, sems.at[3]),
            pltpu.make_async_copy(first_ref, first_out, sems.at[4]),
        ]
        for copy in outputs:
            copy.start()
        for copy in outputs:
            copy.wait()


def finish(count, size, a, x, loads, inverse, first):
    square = pltpu.VMEM(a.shape, F32)
    return pl.pallas_call(
        finish_kernel,
        out_shape=(
            jax.ShapeDtypeStruct(inverse.shape, BF16), jax.ShapeDtypeStruct(first.shape, F32),
        ),
        in_specs=[SMEM, VMEM, ANY, ANY, ANY, ANY, ANY],
        out_specs=(ANY, ANY),
        scratch_shapes=[
            square, square, pltpu.VMEM(loads.shape, F32), pltpu.VMEM(inverse.shape, BF16),
            pltpu.VMEM(first.shape, F32), pltpu.SemaphoreType.DMA((5,)),
        ],
        input_output_aliases={5: 0, 6: 1},
        name="finish",
    )(count, size, a, x, loads, inverse, first)


def sweep_kernel(
    n_sx, n_sy, inv_hbm, first_ref, east_hbm, south_hbm, out_ref, rest_ref, inv_ref, east_ref,
    south_ref, local_sem, own, for_east, for_south,
    got, total, send_sem, recv_sem,
):
    sides = neighbours(n_sx, n_sy)
    loading = [
        pltpu.make_async_copy(east_hbm, east_ref, local_sem.at[0]),
        pltpu.make_async_copy(south_hbm, south_ref, local_sem.at[1]),
        pltpu.make_async_copy(inv_hbm, inv_ref, local_sem.at[2]),
    ]
    for copy in loading:
        copy.start()
    meet(sides)

    halves, span = own.shape[1], own.shape[3]

    def copy_to(sweep, part, side):
        source = (own, own, for_east, for_south)[side]
        return pltpu.make_async_remote_copy(
            src_ref=source.at[sweep, part],
            dst_ref=got.at[sweep, part, (side + 2) % 4],
            send_sem=send_sem.at[sweep, part, side],
            recv_sem=recv_sem.at[sweep, part, (side + 2) % 4],
            device_id=sides[side][1],
            device_id_type=MESH,
        )

    def arrival(sweep, part, side):
        place = got.at[sweep, part, side]
        return pltpu.make_async_remote_copy(
            src_ref=place,
            dst_ref=place,
            send_sem=send_sem.at[sweep, part, side],
            recv_sem=recv_sem.at[sweep, part, side],
            device_id=sides[side][1],
            device_id_type=MESH,
        )

    def send(sweep, part, side):
        @pl.when(sides[side][0])
        def _():
            copy_to(sweep, part, side).start()

    def give_own(sweep, part, coeffs):
        own[sweep, part] = coeffs
        send(sweep, part, 0)
        send(sweep, part, 1)

    def give_products(sweep, part, coeffs):
        for_east[sweep, part] = dot(east_ref[1], coeffs).astype(BF16)
        for_south[sweep, part] = dot(south_ref[1], coeffs).astype(BF16)
        send(sweep, part, 2)
        send(sweep, part, 3)

    def take(sweep, part):
        total[...] = jnp.zeros_like(total)
        for side in (1, 3, 0, 2):
            @pl.when(sides[side][0])
            def _():
                arrival(sweep, part, side).wait_recv()
                value = got[sweep, part, side]
                if side == 2:
                    total[...] += dot(east_ref[0], value)
                elif side == 3:
                    total[...] += dot(south_ref[0], value)
                else:
                    total[...] += value.astype(F32)

    spans = [slice(part * span, (part + 1) * span) for part in range(halves)]
    coeffs = [first_ref[:, at].astype(BF16) for at in spans]
    for part in range(halves):
        give_own(0, part, coeffs[part])
    for copy in loading:
        copy.wait()
    for part in range(halves):
        give_products(0, part, coeffs[part])
    out_ref[...] = (2.0 - damping) * first_ref[...]
    for sweep in range(ITERS - 1):
        for part, at in enumerate(spans):
            take(sweep, part)
            if sweep == ITERS - 2:
                rest_ref[:, at] = total[...].astype(BF16)
                continue
            moved = out_ref[:, at] - damping * dot(inv_ref[...], total[...].astype(BF16))
            coeffs = moved.astype(BF16)
            give_own(sweep + 1, part, coeffs)
            give_products(sweep + 1, part, coeffs)
            out_ref[:, at] = (1.0 - damping) * moved + first_ref[:, at]
    for sweep in range(ITERS - 1):
        for part in range(halves):
            for side in range(4):
                @pl.when(sides[side][0])
                def _():
                    copy_to(sweep, part, side).wait_send()


def settle_kernel(inv_ref, part_ref, rest_ref, out_ref):
    out_ref[...] = part_ref[...] - damping * dot(inv_ref[...], rest_ref[...])


def settle(inverse, part, rest):
    return pl.pallas_call(
        settle_kernel,
        out_shape=jax.ShapeDtypeStruct(part.shape, F32),
        in_specs=[VMEM] * 3,
        out_specs=VMEM,
        name="settle",
    )(inverse, part, rest)


def sweeps_of(n_sx, n_sy, inverse, first, east, south):
    shape = first.shape
    further = ITERS - 1
    halves = 2 if shape[1] % (2 * TILE) == 0 else 1
    piece = (shape[0], shape[1] // halves)
    return pl.pallas_call(
        functools.partial(sweep_kernel, n_sx, n_sy),
        out_shape=(jax.ShapeDtypeStruct(shape, F32), jax.ShapeDtypeStruct(shape, BF16)),
        in_specs=[ANY, VMEM, ANY, ANY],
        out_specs=(VMEM, VMEM),
        scratch_shapes=[
            pltpu.VMEM(inverse.shape, BF16),
            pltpu.VMEM(east.shape, BF16),
            pltpu.VMEM(south.shape, BF16),
            pltpu.SemaphoreType.DMA((3,)),
            pltpu.VMEM((further, halves) + piece, BF16),
            pltpu.VMEM((further, halves) + piece, BF16),
            pltpu.VMEM((further, halves) + piece, BF16),
            pltpu.VMEM((further, halves, 4) + piece, BF16),
            pltpu.VMEM(piece, F32),
            pltpu.SemaphoreType.DMA((further, halves, 4)),
            pltpu.SemaphoreType.DMA((further, halves, 4)),
        ],
        compiler_params=pltpu.CompilerParams(collective_id=0, has_side_effects=True),
        name="sweeps",
    )(inverse, first, east, south)


def solution(mesh):
    n_sx, n_sy = mesh.shape["sx"], mesh.shape["sy"]

    def on_device(basis, diag_weight, correlation_weight, tile_ids, pair_live, loads, load_count):
        basis = basis[0, 0]
        ids = tile_ids[0, 0]
        loads = loads[0, 0]
        a, x, size, inverse, first, block_east, block_south = assemble(
            n_sx, n_sy, ids, pair_live.transpose(0, 2, 1), load_count, basis, correlation_weight[0, 0], diag_weight[0, 0], loads
        )
        inverse, first = finish(load_count, size, a, x, loads, inverse, first)
        part, rest = sweeps_of(n_sx, n_sy, inverse, first, block_east, block_south)
        coeffs = settle(inverse, part, rest)
        return coeffs[None, None]

    return jax.shard_map(
        on_device,
        mesh=mesh,
        in_specs=(
            P("sx", "sy", None, None),
            P("sx", "sy", None),
            P("sx", "sy", None, None),
            P("sx", "sy", None, None),
            P(),
            P("sx", "sy", None, None),
            P("sx", "sy"),
        ),
        out_specs=P("sx", "sy", None, None),
        check_vma=False,
    )
```
